32 devices in a mesh: groups: 2 (over y), tm: 4 (over x, core), tensor: 4 (over z).
Axes of the slice: x: 2, y: 2, z: 4, core: 2. Of those that a mesh axis runs over, the one named last changes fastest.
Arguments:
- start_latent: float32 [256, 128], P(('groups', 'tensor')), parts along dimension 0, may hold values from -6 to 6
- time_index: int32 [8], P(('groups', 'tm')), parts along dimension 0, may hold values from 39 to 998, as said below
- step_weight: int32 [8], P(('groups', 'tm')), parts along dimension 0, may hold values from 1 to 16
- in_weight: bfloat16 [128, 3072], P('tm'), may hold values from -0.5 to 0.5
- mod_weight: bfloat16 [256, 9216], P(None, 'tensor'), may hold values from -0.375 to 0.375
- qkv_weight: bfloat16 [3072, 6144], P(None, 'tensor'), as said below
- out_weight: bfloat16 [2048, 3072], P('tensor'), may hold values from -0.125 to 0.125
- head_weight: bfloat16 [3072, 128], P('tm'), may hold values from -0.109375 to 0.109375
Outputs:
- window_latents: float32 [8, 128, 128], P(('groups', 'tm'), 'tensor'), parts along dimension 0
The draws below stay inside these ranges and needn't reach their ends.
There are 2 independent parts, one for each index of `groups`. The reference program is written for one: setup_inputs(seed, part) draws one part's arguments, and reference() takes and returns one part's arrays. A program takes and returns all parts, laid end to end along the dimension named above; an argument that names none is the same for every part. Nothing has to cross between parts.
Inputs may be any that keep to these rules, and one draw needn't show every extreme that they name: `time_index`: strictly decreasing indices of a 1000-step plan. `qkv_weight`: entries at most 24 / sqrt(3072) in magnitude.
All inputs are finite; a program needn't handle non-finite values.
Results may differ from the reference program's by a relative error of at most 0.0075.
Values may be sent and summed in bfloat16 or wider, within the bound.
A program may use at most 64 MiB of HBM per device.

```python
import math
import jax
import jax.numpy as jnp
from jax import lax

D = 3072
HEADS = 16
HD = 128
C = 128
FREQ = 256
ITERS = 2
TOK = 128
TW = 4


def draw_time_index(key, part):
    spacing = jax.random.randint(jax.random.fold_in(key, 11), (TW,), 1, 960 // TW + 1)
    return (999 - jnp.cumsum(spacing)).astype(jnp.int32)


def draw_qkv_weight(key, part):
    columns = 3 * HEADS * HD
    base_key = jax.random.fold_in(key, 21)
    base = jax.random.truncated_normal(base_key, -4.0, 4.0, (D, columns), jnp.float32)
    chosen = jax.random.permutation(jax.random.fold_in(key, 22), HEADS)[:3]
    column_ids = jnp.arange(columns, dtype=jnp.int32)
    head_of_column = column_ids // (3 * HD)
    role_of_column = column_ids // HD % 3
    factor = jnp.ones((columns,), jnp.float32)
    factor = factor + 2.0 * (head_of_column == chosen[0]).astype(jnp.float32)
    factor = factor + 3.5 * (head_of_column == chosen[1]).astype(jnp.float32)
    factor = factor + 5.0 * (head_of_column == chosen[2]).astype(jnp.float32)
    factor = jnp.where(role_of_column < 2, factor, 1.0)
    return (base * factor[None, :] * float(D) ** (-0.5)).astype(jnp.bfloat16)


def place_ends(result, own_key, smallest, top_value):
    index_at = [jax.random.randint(jax.random.fold_in(own_key, axis), (), 0, length) for axis, length in enumerate(result.shape)]
    main_axis = result.shape.index(max(result.shape))
    neighbour = index_at[:main_axis] + [(index_at[main_axis] + 1) % result.shape[main_axis]] + index_at[main_axis + 1:]
    return result.at[tuple(index_at)].set(smallest).at[tuple(neighbour)].set(top_value)


def block_levels(rng, shape, shards, least, top_value):
    def one(axis_at, parts):
        steps = jax.random.uniform(jax.random.fold_in(jax.random.fold_in(rng, 6), axis_at), (parts,), jnp.float32, least / len(shards), top_value / len(shards))
        return jnp.repeat(jnp.exp(steps), shape[axis_at] // parts).reshape((-1,) + (1,) * (len(shape) - axis_at - 1))

    gain = one(*shards[0])
    for cut in shards[1:]:
        gain = gain * one(*cut)
    return gain


def normal_values(rng, shape, scale, bound, cuts=(), held_as=jnp.bfloat16):
    array = scale * jax.random.normal(rng, shape, jnp.float32)
    if cuts:
        array = array * block_levels(rng, shape, cuts, -0.22, 0.18)
    return jnp.clip(array, -bound, bound).astype(held_as)


def setup_inputs(seed: int = 0, part: int = 0) -> dict:
    keys = jax.random.split(jax.random.key(seed), 9)
    own_keys = jax.random.split(jax.random.fold_in(keys[8], part), 9)
    start_latent = normal_values(own_keys[0], (TOK, C), 1.0, 6.0, ((0, 4),), jnp.float32)
    time_index = draw_time_index(jax.random.fold_in(jax.random.fold_in(keys[8], part), 71), part)
    step_weight = place_ends(jax.random.randint(own_keys[2], (TW,), 1, 17), jax.random.fold_in(own_keys[2], 1), 1, 16).astype(jnp.int32)
    in_weight = normal_values(keys[3], (C, D), C ** -0.5, 0.5, ((0, 4),))
    mod_weight = normal_values(keys[4], (FREQ, 3 * D), FREQ ** -0.5, 0.375, ((1, 4),))
    qkv_weight = draw_qkv_weight(jax.random.fold_in(keys[8], 71), part)
    out_weight = normal_values(keys[6], (HEADS * HD, D), (HEADS * HD) ** -0.5, 0.125, ((0, 4),))
    head_weight = normal_values(keys[7], (D, C), D ** -0.5, 0.109375, ((0, 4),))
    return {"start_latent": start_latent, "time_index": time_index, "step_weight": step_weight, "in_weight": in_weight, "mod_weight": mod_weight, "qkv_weight": qkv_weight, "out_weight": out_weight, "head_weight": head_weight}


NORM_EPS = 1e-06
STEP_DIVISOR = 64.0

def embedding_of(time_index, width):
    half_width = width // 2
    frequency = jnp.exp(-math.log(10000.0) * jnp.arange(half_width).astype(jnp.float32) / half_width)
    angles = time_index.astype(jnp.float32)[:, None] * frequency[None, :]
    return jnp.concatenate([jnp.cos(angles), jnp.sin(angles)], axis=1)

def velocity_of(latents, modulation, in_weight, qkv_weight, out_weight, head_weight):
    shifts = modulation[:D]
    scales = modulation[D:2 * D]
    gate_rows = modulation[2 * D:]
    widened = jnp.dot(latents, in_weight, preferred_element_type=jnp.float32)
    row_mean = lax.optimization_barrier(jnp.mean(widened, axis=1, keepdims=True))
    centered = widened - row_mean
    spread = lax.optimization_barrier(jnp.mean(centered * centered, axis=1, keepdims=True))
    normed = (centered * lax.rsqrt(spread + NORM_EPS) * (1.0 + scales) + shifts).astype(jnp.bfloat16)
    qkv_rows = jnp.dot(normed, qkv_weight, preferred_element_type=jnp.float32).astype(jnp.bfloat16)
    packed = qkv_rows.reshape(TOK, HEADS, 3, HD).astype(jnp.float32)
    scores = jnp.einsum('qhe,khe->hqk', packed[:, :, 0], packed[:, :, 1]) * (1.0 / math.sqrt(HD))
    attention_weights = jax.nn.softmax(scores, axis=-1).astype(jnp.bfloat16)
    attention_weights = lax.optimization_barrier(attention_weights).astype(jnp.float32)
    attended = jnp.einsum('hqk,khe->qhe', attention_weights, packed[:, :, 2]).astype(jnp.bfloat16).reshape(TOK, HEADS * HD)
    scaled_out = (out_weight.astype(jnp.float32) * gate_rows[None, :]).astype(jnp.bfloat16)
    folded = jnp.dot(scaled_out, head_weight, preferred_element_type=jnp.float32).astype(jnp.bfloat16)
    residual = jnp.dot(widened.astype(jnp.bfloat16), head_weight, preferred_element_type=jnp.float32)
    return residual + jnp.dot(attended, folded, preferred_element_type=jnp.float32)

def reference(start_latent, time_index, step_weight, in_weight, mod_weight, qkv_weight, out_weight, head_weight):
    embedding = embedding_of(time_index, FREQ).astype(jnp.bfloat16)
    modulation = jnp.dot(embedding, mod_weight, preferred_element_type=jnp.float32)
    step_size = step_weight.astype(jnp.float32) / STEP_DIVISOR
    guesses = jnp.broadcast_to(start_latent.astype(jnp.bfloat16)[None], (TW, TOK, C))

    def one_timestep(pair):
        return velocity_of(pair[0], pair[1], in_weight, qkv_weight, out_weight, head_weight)
    window_end = start_latent[None]
    for iteration in range(ITERS):
        velocity = lax.map(one_timestep, (guesses, modulation))
        drifts = step_size[:, None, None] * velocity
        window_end = start_latent[None] + jnp.cumsum(drifts, axis=0)
        guesses = (window_end - drifts).astype(jnp.bfloat16)
    return window_end
```

```python
import math

import jax
import jax.numpy as jnp
from jax import lax
from jax.experimental import pallas as pl
from jax.experimental.pallas import tpu as pltpu
from jax.sharding import PartitionSpec as P

D = 3072
HD = 128
ITERS = 2


NORM_EPS = 1e-06
STEP_DIVISOR = 64.0


def carried_in(value, axis, combine, identity):
    devices, index = (lax.axis_size(axis), lax.axis_index(axis))
    everything = lax.all_gather(value, axis)
    start = jnp.broadcast_to(jnp.asarray(identity, value.dtype), value.shape)

    def turn(k, before):
        reached = k < index
        new = combine(before, everything[k])
        return jnp.where(reached, new, before)

    return lax.fori_loop(0, devices, turn, start)


def embedding_of(time_index, width):
    half_width = width // 2
    frequency = jnp.exp(
        -math.log(10000.0) * jnp.arange(half_width).astype(jnp.float32) / half_width
    )
    angles = time_index.astype(jnp.float32)[:, None] * frequency[None, :]
    return jnp.concatenate([jnp.cos(angles), jnp.sin(angles)], axis=1)


def attention(qkv_rows, head_count):
    token_count = qkv_rows.shape[0]
    packed = qkv_rows.reshape(token_count, head_count, 3, HD)
    queries = packed[:, :, 0]
    key_rows = packed[:, :, 1]
    values = packed[:, :, 2]
    block_rows = min(token_count, 512)

    def one_block(block_start):
        scores = jnp.einsum(
            "qhe,khe->hqk", queries, key_rows, preferred_element_type=jnp.float32
        ) * (1.0 / math.sqrt(HD))
        attention_weights = jax.nn.softmax(scores, axis=-1).astype(jnp.bfloat16)
        return jnp.einsum(
            "hqk,khe->qhe", attention_weights, values, preferred_element_type=jnp.float32
        ).astype(jnp.bfloat16)

    block_starts = jnp.arange(token_count // block_rows, dtype=jnp.int32) * block_rows
    blocks_out = lax.map(one_block, block_starts)
    return blocks_out.reshape(token_count, head_count * HD)


def evaluate(latents, shifts, scales, folded, in_weight_all, qkv_weight, head_count):
    widened = jnp.dot(latents, in_weight_all, preferred_element_type=jnp.float32)
    row_mean = jnp.mean(widened, axis=1, keepdims=True)
    centered = widened - row_mean
    spread = jnp.mean(centered * centered, axis=1, keepdims=True)
    normed = (centered * lax.rsqrt(spread + NORM_EPS) * (1.0 + scales) + shifts).astype(
        jnp.bfloat16
    )
    qkv_rows = jnp.dot(normed, qkv_weight, preferred_element_type=jnp.float32).astype(jnp.bfloat16)
    attended = attention(qkv_rows, head_count)
    return (widened, jnp.dot(attended, folded, preferred_element_type=jnp.float32))


def fold_head(out_weight, gate_rows, head_weight_all):
    scaled_out = (out_weight.astype(jnp.float32) * gate_rows[None, :]).astype(jnp.bfloat16)
    return jnp.dot(scaled_out, head_weight_all, preferred_element_type=jnp.float32).astype(
        jnp.bfloat16
    )


def add_terms(earlier, later):
    return earlier + later


def local(
    start_latent,
    time_index,
    step_weight,
    in_weight,
    mod_weight,
    qkv_weight,
    out_weight,
    head_weight,
):
    rows_dev = start_latent.shape[0]
    head_count = qkv_weight.shape[1] // (3 * HD)
    in_weight_all, head_weight_all = (
        lax.all_gather(in_weight, "tm", axis=0, tiled=True),
        lax.all_gather(head_weight, "tm", axis=0, tiled=True),
    )
    embedding = embedding_of(time_index, mod_weight.shape[0]).astype(jnp.bfloat16)
    mod_part = jnp.dot(embedding, mod_weight, preferred_element_type=jnp.float32)
    modulation = lax.all_gather(mod_part, "tensor", axis=1, tiled=True)
    shifts = modulation[:, :D]
    scales = modulation[:, D : 2 * D]
    gate_rows = modulation[:, 2 * D :]
    folded = fold_head(out_weight, gate_rows[0], head_weight_all)
    step_size = step_weight.astype(jnp.float32) / STEP_DIVISOR
    start_all = lax.all_gather(start_latent, "tensor", axis=0, tiled=True)
    row_first = lax.axis_index("tensor") * rows_dev
    guesses = start_all.astype(jnp.bfloat16)[None]
    window_end = start_latent[None]
    for iteration in range(ITERS):
        widened, partial_sum = evaluate(
            guesses[0], shifts[0], scales[0], folded, in_weight_all, qkv_weight, head_count
        )
        widened_list = [widened]
        partials = [partial_sum]
        stacked = jnp.stack(partials, 0)
        residual = jnp.stack(
            [
                jnp.dot(
                    lax.dynamic_slice_in_dim(widened, row_first, rows_dev, 0).astype(jnp.bfloat16),
                    head_weight_all,
                    preferred_element_type=jnp.float32,
                )
                for widened in widened_list
            ],
            0,
        )
        velocity = lax.psum_scatter(stacked, "tensor", scatter_dimension=1, tiled=True) + residual
        drifts = step_size[:, None, None] * velocity
        inclusive = jnp.cumsum(drifts, axis=0)
        earlier = carried_in(inclusive[-1], "tm", add_terms, jnp.zeros_like(inclusive[-1]))
        window_end = start_latent[None] + earlier[None] + inclusive
        if iteration + 1 < ITERS:
            guesses = lax.all_gather(
                (window_end - drifts).astype(jnp.bfloat16), "tensor", axis=1, tiled=True
            )
    return window_end


MESH = pl.DeviceIdType.MESH


def fused_kernel(
    tm_size,
    tensor_size,
    start_ref,
    time_ref,
    step_ref,
    in_ref,
    mod_ref,
    qkv_ref,
    out_w_ref,
    head_ref,
    o_ref,
    mod_v,
    qkv_v,
    out_v,
    in_v,
    head_v,
    mods,
    centered_v,
    scaled_v,
    table_v,
    shift_v,
    folded_v,
    guess_v,
    own_v,
    part_v,
    landed_v,
    drift_v,
    drifts_v,
    local_sem,
    in_send,
    in_recv,
    head_send,
    head_recv,
    mod_send,
    mod_recv,
    guess_send,
    guess_recv,
    part_send,
    part_recv,
    drift_send,
    drift_recv,
):
    me = lax.axis_index("tm")
    mine = lax.axis_index("tensor")
    chips = tm_size // 2
    chip, core = me // 2, lax.rem(me, 2)
    partner = chip * 2 + (1 - core)
    rows = start_ref.shape[0]
    channels = start_ref.shape[1]
    in_rows = in_ref.shape[0]
    head_rows = head_ref.shape[0]
    heads = qkv_ref.shape[1] // (3 * HD)

    barrier = pltpu.get_barrier_semaphore()
    for k in range(1, tm_size):
        pl.semaphore_signal(
            barrier, inc=1, device_id={"tm": lax.rem(me + k, tm_size)}, device_id_type=MESH
        )
    for k in range(1, tensor_size):
        pl.semaphore_signal(
            barrier,
            inc=1,
            device_id={"tensor": lax.rem(mine + k, tensor_size)},
            device_id_type=MESH,
        )

    def row_block(ref, index, count):
        return ref.at[pl.ds(pl.multiple_of(index * count, count), count)]

    copy_mod = pltpu.make_async_copy(mod_ref, mod_v, local_sem.at[0])
    copy_in = pltpu.make_async_copy(in_ref, row_block(in_v, me, in_rows), local_sem.at[1])
    copy_head = pltpu.make_async_copy(head_ref, row_block(head_v, me, head_rows), local_sem.at[2])
    copy_out = pltpu.make_async_copy(out_w_ref, out_v, local_sem.at[3])
    copy_qkv = pltpu.make_async_copy(qkv_ref, qkv_v, local_sem.at[4])
    for copy in (copy_mod, copy_in, copy_head, copy_out, copy_qkv):
        copy.start()
    pl.semaphore_wait(barrier, tm_size - 1 + tensor_size - 1)

    def to_tm(src, dst, send, recv, target):
        return pltpu.make_async_remote_copy(
            src_ref=src,
            dst_ref=dst,
            send_sem=send,
            recv_sem=recv,
            device_id={"tm": target},
            device_id_type=MESH,
        )

    def to_tensor(src, dst, send, recv, target):
        return pltpu.make_async_remote_copy(
            src_ref=src,
            dst_ref=dst,
            send_sem=send,
            recv_sem=recv,
            device_id={"tensor": target},
            device_id_type=MESH,
        )

    def start_gather(source, full, count, send, recv):
        started = []
        for k in range(1, chips):
            target = lax.rem(chip + k, chips) * 2 + core
            started.append(
                to_tm(source, row_block(full, me, count), send.at[k], recv.at[k], target)
            )
        started.append(
            to_tm(source, row_block(full, me, count), send.at[0], recv.at[0], partner)
        )
        for copy in started:
            copy.start()
        return started

    def relay_gather(full, count, send, recv):
        started = []
        for k in range(1, chips):
            source = lax.rem(chip + chips - k, chips) * 2 + core
            block = row_block(full, source, count)
            to_tm(block, block, send.at[k], recv.at[k], partner).wait_recv()
            relay = to_tm(block, block, send.at[chips + k], recv.at[chips + k], partner)
            relay.start()
            started.append(relay)
        return started

    def end_gather(full, count, send, recv):
        block = row_block(full, partner, count)
        to_tm(block, block, send.at[0], recv.at[0], partner).wait_recv()
        for k in range(1, chips):
            source = lax.rem(chip + chips - k, chips) * 2 + (1 - core)
            block = row_block(full, source, count)
            to_tm(block, block, send.at[k], recv.at[chips + k], partner).wait_recv()

    def share(buffer, send, recv):
        started = []
        for k in range(1, tensor_size):
            block = buffer.at[mine]
            copy = to_tensor(
                block, block, send.at[k], recv.at[k], lax.rem(mine + k, tensor_size)
            )
            copy.start()
            started.append(copy)
        return started

    def shared(buffer, send, recv):
        for k in range(1, tensor_size):
            block = buffer.at[lax.rem(mine + tensor_size - k, tensor_size)]
            to_tensor(block, block, send.at[k], recv.at[k], mine).wait_recv()

    sends = []
    sends += start_gather(in_ref, in_v, in_rows, in_send, in_recv)
    sends += start_gather(head_ref, head_v, head_rows, head_send, head_recv)

    start_own = start_ref[...]
    own_v[...] = start_own.astype(jnp.bfloat16)
    guess_v[0, mine] = start_own.astype(jnp.bfloat16)
    sends += share(guess_v.at[0], guess_send.at[0], guess_recv.at[0])

    half = mod_ref.shape[0] // 2
    order = lax.broadcasted_iota(jnp.int32, (8, half), 1).astype(jnp.float32)
    frequency = jnp.exp(-math.log(10000.0) * order / half)
    angles = time_ref[0].astype(jnp.float32) * frequency
    embedding = jnp.concatenate([jnp.cos(angles), jnp.sin(angles)], axis=1).astype(jnp.bfloat16)
    copy_mod.wait()
    mod_part = jnp.dot(embedding, mod_v[...], preferred_element_type=jnp.float32)
    mods[mine] = mod_part[0:1]
    sends += share(mods, mod_send, mod_recv)

    copy_in.wait()
    sends += relay_gather(in_v, in_rows, in_send, in_recv)
    shared(mods, mod_send, mod_recv)
    modulation = jnp.concatenate([mods[k] for k in range(tensor_size)], axis=1)
    shifts = modulation[:, :D]
    scales = 1.0 + modulation[:, D : 2 * D]
    gates = modulation[:, 2 * D :]
    copy_out.wait()
    step_rows = 128
    for r in range(0, out_v.shape[0], step_rows):
        out_v[r : r + step_rows] = (
            out_v[r : r + step_rows].astype(jnp.float32) * gates
        ).astype(jnp.bfloat16)

    high = shifts.astype(jnp.bfloat16)
    low = (shifts - high.astype(jnp.float32)).astype(jnp.bfloat16)
    row_id = lax.broadcasted_iota(jnp.int32, (16, D), 0)
    pair = jnp.where(
        row_id == 0,
        high.astype(jnp.float32),
        jnp.where(row_id == 1, low.astype(jnp.float32), 0.0),
    )
    scaled_v[channels : channels + 16] = pair.astype(jnp.bfloat16)

    end_gather(in_v, in_rows, in_send, in_recv)
    for r in range(0, channels, 32):
        block = in_v[r : r + 32].astype(jnp.float32)
        block = block - jnp.mean(block, axis=1, keepdims=True)
        centered_v[r : r + 32] = block.astype(jnp.bfloat16)
        scaled_v[r : r + 32] = (block * scales).astype(jnp.bfloat16)

    copy_qkv.wait()
    for h in range(heads):
        columns = slice(3 * HD * h, 3 * HD * (h + 1))
        product = jnp.dot(
            scaled_v[...], qkv_v[:, columns], preferred_element_type=jnp.float32
        )
        main = product[:channels]
        main_high = main.astype(jnp.bfloat16)
        table_v[:channels, columns] = main_high
        table_v[channels:, columns] = (main - main_high.astype(jnp.float32)).astype(jnp.bfloat16)
        shift_v[:, columns] = product[channels : channels + 1] + product[channels + 1 : channels + 2]
    centered = centered_v[...]
    spread_table = lax.dot_general(
        centered, centered, (((1,), (1,)), ((), ())), preferred_element_type=jnp.float32
    ) * (1.0 / D)
    spread_high = spread_table.astype(jnp.bfloat16)
    spread_low = (spread_table - spread_high.astype(jnp.float32)).astype(jnp.bfloat16)
    spread_pair = jnp.concatenate([spread_high, spread_low], axis=0)

    sends += relay_gather(head_v, head_rows, head_send, head_recv)
    copy_head.wait()
    shared(guess_v.at[0], guess_send.at[0], guess_recv.at[0])

    step_size = step_ref[0].astype(jnp.float32) / STEP_DIVISOR
    residual_pair = None
    for iteration in range(ITERS):
        guess = jnp.concatenate([guess_v[iteration, k] for k in range(tensor_size)], axis=0)
        twice = jnp.concatenate([guess, guess], axis=1)
        spread = jnp.sum(
            jnp.dot(twice, spread_pair, preferred_element_type=jnp.float32)
            * guess.astype(jnp.float32),
            axis=1,
            keepdims=True,
        )
        inverse = lax.rsqrt(jnp.maximum(spread, 0.0) + NORM_EPS)
        qkv_rows = jnp.dot(twice, table_v[...], preferred_element_type=jnp.float32)
        qkv_rows = (qkv_rows * inverse + shift_v[...]).astype(jnp.bfloat16)
        attended = []
        for h in range(heads):
            first = 3 * HD * h
            query = qkv_rows[:, first : first + HD]
            key = qkv_rows[:, first + HD : first + 2 * HD]
            value = qkv_rows[:, first + 2 * HD : first + 3 * HD]
            scores = lax.dot_general(
                query, key, (((1,), (1,)), ((), ())), preferred_element_type=jnp.float32
            ) * (1.0 / math.sqrt(HD))
            scores = jnp.exp(scores - jnp.max(scores, axis=1, keepdims=True))
            probs = (scores / jnp.sum(scores, axis=1, keepdims=True)).astype(jnp.bfloat16)
            attended.append(
                jnp.dot(probs, value, preferred_element_type=jnp.float32).astype(jnp.bfloat16)
            )
        if iteration == 0:
            end_gather(head_v, head_rows, head_send, head_recv)
            folded_v[...] = jnp.dot(
                out_v[...], head_v[...], preferred_element_type=jnp.float32
            ).astype(jnp.bfloat16)
            residual_table = jnp.dot(in_v[...], head_v[...], preferred_element_type=jnp.float32)
            residual_high = residual_table.astype(jnp.bfloat16)
            residual_low = (residual_table - residual_high.astype(jnp.float32)).astype(
                jnp.bfloat16
            )
            residual_pair = jnp.concatenate([residual_high, residual_low], axis=0)
        partial = jnp.dot(
            jnp.concatenate(attended, axis=1), folded_v[...], preferred_element_type=jnp.float32
        )
        part_v[iteration] = partial.reshape(tensor_size, rows, channels)
        for k in range(1, tensor_size):
            target = lax.rem(mine + k, tensor_size)
            copy = to_tensor(
                part_v.at[iteration, target],
                landed_v.at[iteration, k],
                part_send.at[iteration, k],
                part_recv.at[iteration, k],
                target,
            )
            copy.start()
            sends.append(copy)
        own = own_v[...] if iteration == 0 else guess_v[iteration, mine]
        velocity = jnp.dot(
            jnp.concatenate([own, own], axis=1), residual_pair, preferred_element_type=jnp.float32
        )
        velocity = velocity + part_v[iteration, mine]
        for k in range(1, tensor_size):
            to_tensor(
                part_v.at[iteration, mine],
                landed_v.at[iteration, k],
                part_send.at[iteration, k],
                part_recv.at[iteration, k],
                mine,
            ).wait_recv()
            velocity = velocity + landed_v[iteration, k]
        drift = step_size * velocity
        drift_v[iteration] = drift
        for k in range(1, tm_size):
            copy = to_tm(
                drift_v.at[iteration],
                drifts_v.at[iteration, k],
                drift_send.at[iteration, k],
                drift_recv.at[iteration, k],
                lax.rem(me + k, tm_size),
            )
            copy.start()
            sends.append(copy)
        window = start_own
        for k in range(1, tm_size):
            to_tm(
                drift_v.at[iteration],
                drifts_v.at[iteration, k],
                drift_send.at[iteration, k],
                drift_recv.at[iteration, k],
                me,
            ).wait_recv()
            reached = jnp.where(k <= me, 1.0, 0.0)
            window = window + jnp.where(reached > 0.5, drifts_v[iteration, k], 0.0)
        if iteration + 1 < ITERS:
            guess_v[iteration + 1, mine] = window.astype(jnp.bfloat16)
            later = iteration + 1
            sends += share(guess_v.at[later], guess_send.at[later], guess_recv.at[later])
            shared(guess_v.at[later], guess_send.at[later], guess_recv.at[later])
        else:
            o_ref[0] = window + drift
    for copy in sends:
        copy.wait_send()


def fused(tm_size, tensor_size, *arrays):
    start, _, _, in_w, mod_w, qkv_w, out_w, head_w = arrays
    rows, channels = start.shape
    bf16, f32 = jnp.bfloat16, jnp.float32
    dma = pltpu.SemaphoreType.DMA
    anywhere = pl.BlockSpec(memory_space=pl.ANY)
    scalar = pl.BlockSpec(memory_space=pltpu.SMEM)
    vector = pl.BlockSpec(memory_space=pltpu.VMEM)
    return pl.pallas_call(
        lambda *refs: fused_kernel(tm_size, tensor_size, *refs),
        name="picard",
        out_shape=jax.ShapeDtypeStruct((1, rows, channels), f32),
        in_specs=[vector, scalar, scalar] + [anywhere] * 5,
        out_specs=vector,
        scratch_shapes=[
            pltpu.VMEM(mod_w.shape, bf16),
            pltpu.VMEM(qkv_w.shape, bf16),
            pltpu.VMEM(out_w.shape, bf16),
            pltpu.VMEM((channels, D), bf16),
            pltpu.VMEM((D, channels), bf16),
            pltpu.VMEM((tensor_size, 1, mod_w.shape[1]), f32),
            pltpu.VMEM((channels, D), bf16),
            pltpu.VMEM((channels + 16, D), bf16),
            pltpu.VMEM((2 * channels, qkv_w.shape[1]), bf16),
            pltpu.VMEM((1, qkv_w.shape[1]), f32),
            pltpu.VMEM((out_w.shape[0], channels), bf16),
            pltpu.VMEM((ITERS, tensor_size, rows, channels), bf16),
            pltpu.VMEM((rows, channels), bf16),
            pltpu.VMEM((ITERS, tensor_size, rows, channels), f32),
            pltpu.VMEM((ITERS, tensor_size, rows, channels), f32),
            pltpu.VMEM((ITERS, rows, channels), f32),
            pltpu.VMEM((ITERS, tm_size, rows, channels), f32),
            dma((5,)),
            dma((tm_size,)),
            dma((tm_size,)),
            dma((tm_size,)),
            dma((tm_size,)),
            dma((tensor_size,)),
            dma((tensor_size,)),
            dma((ITERS, tensor_size)),
            dma((ITERS, tensor_size)),
            dma((ITERS, tensor_size)),
            dma((ITERS, tensor_size)),
            dma((ITERS, tm_size)),
            dma((ITERS, tm_size)),
        ],
        compiler_params=pltpu.CompilerParams(
            collective_id=0, has_side_effects=True, vmem_limit_bytes=48 * 1024 * 1024
        ),
    )(*arrays)


def aligned(tm_size, tensor_size, arrays):
    start, times, _, in_w, mod_w, qkv_w, out_w, head_w = arrays
    return (
        times.shape[0] == 1
        and tm_size % 2 == 0
        and in_w.shape[0] % 16 == 0
        and head_w.shape[0] % 16 == 0
        and start.shape[0] % 16 == 0
        and mod_w.shape[1] % 128 == 0
        and out_w.shape[0] % 128 == 0
    )


def device_program(tm_size, tensor_size):
    def run(*arrays):
        if aligned(tm_size, tensor_size, arrays):
            return fused(tm_size, tensor_size, *arrays)
        return local(*arrays)

    return run


def solution(mesh):
    return jax.shard_map(
        device_program(mesh.shape["tm"], mesh.shape["tensor"]),
        mesh=mesh,
        in_specs=(
            P(("groups", "tensor"), None),
            P(("groups", "tm")),
            P(("groups", "tm")),
            P("tm", None),
            P(None, "tensor"),
            P(None, "tensor"),
            P("tensor", None),
            P("tm", None),
        ),
        out_specs=P(("groups", "tm"), "tensor", None),
        check_vma=False,
    )
```

```python
import math

import jax
import jax.numpy as jnp
from jax import lax
from jax.experimental import pallas as pl
from jax.experimental.pallas import tpu as pltpu
from jax.sharding import PartitionSpec as P

D = 3072
HD = 128
ITERS = 2


NORM_EPS = 1e-06
STEP_DIVISOR = 64.0


def carried_in(value, axis, combine, identity):
    devices, index = (lax.axis_size(axis), lax.axis_index(axis))
    everything = lax.all_gather(value, axis)
    start = jnp.broadcast_to(jnp.asarray(identity, value.dtype), value.shape)

    def turn(k, before):
        reached = k < index
        new = combine(before, everything[k])
        return jnp.where(reached, new, before)

    return lax.fori_loop(0, devices, turn, start)


def embedding_of(time_index, width):
    half_width = width // 2
    frequency = jnp.exp(
        -math.log(10000.0) * jnp.arange(half_width).astype(jnp.float32) / half_width
    )
    angles = time_index.astype(jnp.float32)[:, None] * frequency[None, :]
    return jnp.concatenate([jnp.cos(angles), jnp.sin(angles)], axis=1)


def attention(qkv_rows, head_count):
    token_count = qkv_rows.shape[0]
    packed = qkv_rows.reshape(token_count, head_count, 3, HD)
    queries = packed[:, :, 0]
    key_rows = packed[:, :, 1]
    values = packed[:, :, 2]
    block_rows = min(token_count, 512)

    def one_block(block_start):
        scores = jnp.einsum(
            "qhe,khe->hqk", queries, key_rows, preferred_element_type=jnp.float32
        ) * (1.0 / math.sqrt(HD))
        attention_weights = jax.nn.softmax(scores, axis=-1).astype(jnp.bfloat16)
        return jnp.einsum(
            "hqk,khe->qhe", attention_weights, values, preferred_element_type=jnp.float32
        ).astype(jnp.bfloat16)

    block_starts = jnp.arange(token_count // block_rows, dtype=jnp.int32) * block_rows
    blocks_out = lax.map(one_block, block_starts)
    return blocks_out.reshape(token_count, head_count * HD)


def evaluate(latents, shifts, scales, folded, in_weight_all, qkv_weight, head_count):
    widened = jnp.dot(latents, in_weight_all, preferred_element_type=jnp.float32)
    row_mean = jnp.mean(widened, axis=1, keepdims=True)
    centered = widened - row_mean
    spread = jnp.mean(centered * centered, axis=1, keepdims=True)
    normed = (centered * lax.rsqrt(spread + NORM_EPS) * (1.0 + scales) + shifts).astype(
        jnp.bfloat16
    )
    qkv_rows = jnp.dot(normed, qkv_weight, preferred_element_type=jnp.float32).astype(jnp.bfloat16)
    attended = attention(qkv_rows, head_count)
    return (widened, jnp.dot(attended, folded, preferred_element_type=jnp.float32))


def fold_head(out_weight, gate_rows, head_weight_all):
    scaled_out = (out_weight.astype(jnp.float32) * gate_rows[None, :]).astype(jnp.bfloat16)
    return jnp.dot(scaled_out, head_weight_all, preferred_element_type=jnp.float32).astype(
        jnp.bfloat16
    )


def add_terms(earlier, later):
    return earlier + later


def local(
    start_latent,
    time_index,
    step_weight,
    in_weight,
    mod_weight,
    qkv_weight,
    out_weight,
    head_weight,
):
    rows_dev = start_latent.shape[0]
    head_count = qkv_weight.shape[1] // (3 * HD)
    in_weight_all, head_weight_all = (
        lax.all_gather(in_weight, "tm", axis=0, tiled=True),
        lax.all_gather(head_weight, "tm", axis=0, tiled=True),
    )
    embedding = embedding_of(time_index, mod_weight.shape[0]).astype(jnp.bfloat16)
    mod_part = jnp.dot(embedding, mod_weight, preferred_element_type=jnp.float32)
    modulation = lax.all_gather(mod_part, "tensor", axis=1, tiled=True)
    shifts = modulation[:, :D]
    scales = modulation[:, D : 2 * D]
    gate_rows = modulation[:, 2 * D :]
    folded = fold_head(out_weight, gate_rows[0], head_weight_all)
    step_size = step_weight.astype(jnp.float32) / STEP_DIVISOR
    start_all = lax.all_gather(start_latent, "tensor", axis=0, tiled=True)
    row_first = lax.axis_index("tensor") * rows_dev
    guesses = start_all.astype(jnp.bfloat16)[None]
    window_end = start_latent[None]
    for iteration in range(ITERS):
        widened, partial_sum = evaluate(
            guesses[0], shifts[0], scales[0], folded, in_weight_all, qkv_weight, head_count
        )
        widened_list = [widened]
        partials = [partial_sum]
        stacked = jnp.stack(partials, 0)
        residual = jnp.stack(
            [
                jnp.dot(
                    lax.dynamic_slice_in_dim(widened, row_first, rows_dev, 0).astype(jnp.bfloat16),
                    head_weight_all,
                    preferred_element_type=jnp.float32,
                )
                for widened in widened_list
            ],
            0,
        )
        velocity = lax.psum_scatter(stacked, "tensor", scatter_dimension=1, tiled=True) + residual
        drifts = step_size[:, None, None] * velocity
        inclusive = jnp.cumsum(drifts, axis=0)
        earlier = carried_in(inclusive[-1], "tm", add_terms, jnp.zeros_like(inclusive[-1]))
        window_end = start_latent[None] + earlier[None] + inclusive
        if iteration + 1 < ITERS:
            guesses = lax.all_gather(
                (window_end - drifts).astype(jnp.bfloat16), "tensor", axis=1, tiled=True
            )
    return window_end


MESH = pl.DeviceIdType.MESH


def fused_kernel(
    tm_size,
    tensor_size,
    start_ref,
    time_ref,
    step_ref,
    in_ref,
    mod_ref,
    qkv_ref,
    out_w_ref,
    head_ref,
    o_ref,
    mod_v,
    qkv_v,
    out_v,
    in_v,
    head_v,
    mods,
    centered_v,
    scaled_v,
    table_v,
    shift_v,
    folded_v,
    guess_v,
    own_v,
    part_v,
    landed_v,
    whole_v,
    start_v,
    time_s,
    step_s,
    local_sem,
    in_send,
    in_recv,
    head_send,
    head_recv,
    mod_send,
    mod_recv,
    guess_send,
    guess_recv,
    part_send,
    part_recv,
):
    me = lax.axis_index("tm")
    mine = lax.axis_index("tensor")
    chips = tm_size // 2
    chip, core = me // 2, lax.rem(me, 2)
    partner = chip * 2 + (1 - core)
    rows = start_ref.shape[0]
    channels = start_ref.shape[1]
    in_rows = in_ref.shape[0]
    head_rows = head_ref.shape[0]
    heads = qkv_ref.shape[1] // (3 * HD)

    barrier = pltpu.get_barrier_semaphore()
    peers = [(a, b) for a in range(tm_size) for b in range(tensor_size)][1:]
    for a, b in peers:
        pl.semaphore_signal(
            barrier,
            inc=1,
            device_id={
                "tm": lax.rem(me + a, tm_size),
                "tensor": lax.rem(mine + b, tensor_size),
            },
            device_id_type=MESH,
        )

    def row_block(ref, index, count):
        return ref.at[pl.ds(pl.multiple_of(index * count, count), count)]

    copy_mod = pltpu.make_async_copy(mod_ref, mod_v, local_sem.at[0])
    copy_in = pltpu.make_async_copy(in_ref, row_block(in_v, me, in_rows), local_sem.at[1])
    copy_head = pltpu.make_async_copy(head_ref, row_block(head_v, me, head_rows), local_sem.at[2])
    copy_out = pltpu.make_async_copy(out_w_ref, out_v, local_sem.at[3])
    copy_qkv = pltpu.make_async_copy(qkv_ref, qkv_v, local_sem.at[4])
    copy_start = pltpu.make_async_copy(start_ref, start_v, local_sem.at[5])
    copy_time = pltpu.make_async_copy(time_ref, time_s, local_sem.at[6])
    copy_step = pltpu.make_async_copy(step_ref, step_s, local_sem.at[7])
    for copy in (copy_time, copy_step, copy_start, copy_mod, copy_in, copy_head, copy_out, copy_qkv):
        copy.start()
    pl.semaphore_wait(barrier, len(peers))

    def to_tm(src, dst, send, recv, target):
        return pltpu.make_async_remote_copy(
            src_ref=src,
            dst_ref=dst,
            send_sem=send,
            recv_sem=recv,
            device_id={"tm": target},
            device_id_type=MESH,
        )

    def to_tensor(src, dst, send, recv, target):
        return pltpu.make_async_remote_copy(
            src_ref=src,
            dst_ref=dst,
            send_sem=send,
            recv_sem=recv,
            device_id={"tensor": target},
            device_id_type=MESH,
        )

    def start_gather(source, full, count, send, recv):
        started = []
        for k in range(1, chips):
            target = lax.rem(chip + k, chips) * 2 + core
            started.append(
                to_tm(source, row_block(full, me, count), send.at[k], recv.at[k], target)
            )
        started.append(
            to_tm(source, row_block(full, me, count), send.at[0], recv.at[0], partner)
        )
        for copy in started:
            copy.start()
        return started

    def relay_gather(full, count, send, recv):
        started = []
        for k in range(1, chips):
            source = lax.rem(chip + chips - k, chips) * 2 + core
            block = row_block(full, source, count)
            to_tm(block, block, send.at[k], recv.at[k], partner).wait_recv()
            relay = to_tm(block, block, send.at[chips + k], recv.at[chips + k], partner)
            relay.start()
            started.append(relay)
        return started

    def end_gather(full, count, send, recv):
        block = row_block(full, partner, count)
        to_tm(block, block, send.at[0], recv.at[0], partner).wait_recv()
        for k in range(1, chips):
            source = lax.rem(chip + chips - k, chips) * 2 + (1 - core)
            block = row_block(full, source, count)
            to_tm(block, block, send.at[k], recv.at[chips + k], partner).wait_recv()

    def share(buffer, send, recv):
        started = []
        for k in range(1, tensor_size):
            block = buffer.at[mine]
            copy = to_tensor(
                block, block, send.at[k], recv.at[k], lax.rem(mine + k, tensor_size)
            )
            copy.start()
            started.append(copy)
        return started

    def shared(buffer, send, recv):
        for k in range(1, tensor_size):
            block = buffer.at[lax.rem(mine + tensor_size - k, tensor_size)]
            to_tensor(block, block, send.at[k], recv.at[k], mine).wait_recv()

    sends = []
    sends += start_gather(in_ref, in_v, in_rows, in_send, in_recv)
    sends += start_gather(head_ref, head_v, head_rows, head_send, head_recv)

    copy_start.wait()
    start_own = start_v[...]
    own_v[...] = start_own.astype(jnp.bfloat16)
    guess_v[0, mine] = start_own.astype(jnp.bfloat16)
    sends += share(guess_v.at[0], guess_send.at[0], guess_recv.at[0])

    half = mod_ref.shape[0] // 2
    order = lax.broadcasted_iota(jnp.int32, (8, half), 1).astype(jnp.float32)
    frequency = jnp.exp(-math.log(10000.0) * order / half)
    copy_time.wait()
    angles = time_s[0].astype(jnp.float32) * frequency
    embedding = jnp.concatenate([jnp.cos(angles), jnp.sin(angles)], axis=1).astype(jnp.bfloat16)
    copy_mod.wait()
    mod_part = jnp.dot(embedding, mod_v[...], preferred_element_type=jnp.float32)
    mods[mine] = mod_part[0:1]
    sends += share(mods, mod_send, mod_recv)

    copy_in.wait()
    sends += relay_gather(in_v, in_rows, in_send, in_recv)
    shared(mods, mod_send, mod_recv)
    modulation = jnp.concatenate([mods[k] for k in range(tensor_size)], axis=1)
    shifts = modulation[:, :D]
    scales = 1.0 + modulation[:, D : 2 * D]
    gates = modulation[:, 2 * D :]
    copy_out.wait()
    step_rows = 128
    for r in range(0, out_v.shape[0], step_rows):
        out_v[r : r + step_rows] = (
            out_v[r : r + step_rows].astype(jnp.float32) * gates
        ).astype(jnp.bfloat16)

    high = shifts.astype(jnp.bfloat16)
    low = (shifts - high.astype(jnp.float32)).astype(jnp.bfloat16)
    row_id = lax.broadcasted_iota(jnp.int32, (16, D), 0)
    pair = jnp.where(
        row_id == 0,
        high.astype(jnp.float32),
        jnp.where(row_id == 1, low.astype(jnp.float32), 0.0),
    )
    scaled_v[channels : channels + 16] = pair.astype(jnp.bfloat16)

    end_gather(in_v, in_rows, in_send, in_recv)
    for r in range(0, channels, 32):
        block = in_v[r : r + 32].astype(jnp.float32)
        block = block - jnp.mean(block, axis=1, keepdims=True)
        centered_v[r : r + 32] = block.astype(jnp.bfloat16)
        scaled_v[r : r + 32] = (block * scales).astype(jnp.bfloat16)

    centered = centered_v[...]
    spread_table = lax.dot_general(
        centered, centered, (((1,), (1,)), ((), ())), preferred_element_type=jnp.float32
    ) * (1.0 / D)
    spread_high = spread_table.astype(jnp.bfloat16)
    spread_low = (spread_table - spread_high.astype(jnp.float32)).astype(jnp.bfloat16)
    spread_pair = jnp.concatenate([spread_high, spread_low], axis=0)

    copy_qkv.wait()
    for h in range(heads):
        if h == heads - 1:
            sends += relay_gather(head_v, head_rows, head_send, head_recv)
        columns = slice(3 * HD * h, 3 * HD * (h + 1))
        product = jnp.dot(
            scaled_v[...], qkv_v[:, columns], preferred_element_type=jnp.float32
        )
        main = product[:channels]
        main_high = main.astype(jnp.bfloat16)
        table_v[:channels, columns] = main_high
        table_v[channels:, columns] = (main - main_high.astype(jnp.float32)).astype(jnp.bfloat16)
        shift_v[:, columns] = product[channels : channels + 1] + product[channels + 1 : channels + 2]
    copy_head.wait()
    shared(guess_v.at[0], guess_send.at[0], guess_recv.at[0])

    copy_step.wait()
    step_size = step_s[0].astype(jnp.float32) / STEP_DIVISOR
    residual_pair = None
    for iteration in range(ITERS):
        guess = jnp.concatenate([guess_v[iteration, k] for k in range(tensor_size)], axis=0)
        twice = jnp.concatenate([guess, guess], axis=1)
        spread = jnp.sum(
            jnp.dot(twice, spread_pair, preferred_element_type=jnp.float32)
            * guess.astype(jnp.float32),
            axis=1,
            keepdims=True,
        )
        inverse = lax.rsqrt(jnp.maximum(spread, 0.0) + NORM_EPS)
        qkv_rows = jnp.dot(twice, table_v[...], preferred_element_type=jnp.float32)
        qkv_rows = (qkv_rows * inverse + shift_v[...]).astype(jnp.bfloat16)
        attended = []
        for h in range(heads):
            first = 3 * HD * h
            query = qkv_rows[:, first : first + HD]
            key = qkv_rows[:, first + HD : first + 2 * HD]
            value = qkv_rows[:, first + 2 * HD : first + 3 * HD]
            scores = lax.dot_general(
                query, key, (((1,), (1,)), ((), ())), preferred_element_type=jnp.float32
            ) * (1.0 / math.sqrt(HD))
            scores = jnp.exp(scores - jnp.max(scores, axis=1, keepdims=True))
            probs = (scores / jnp.sum(scores, axis=1, keepdims=True)).astype(jnp.bfloat16)
            attended.append(
                jnp.dot(probs, value, preferred_element_type=jnp.float32).astype(jnp.bfloat16)
            )
        if iteration == 0:
            end_gather(head_v, head_rows, head_send, head_recv)
            folded_v[...] = jnp.dot(
                out_v[...], head_v[...], preferred_element_type=jnp.float32
            ).astype(jnp.bfloat16)
        partial = jnp.dot(
            jnp.concatenate(attended, axis=1), folded_v[...], preferred_element_type=jnp.float32
        )
        if iteration == 0:
            residual_table = jnp.dot(in_v[...], head_v[...], preferred_element_type=jnp.float32)
            residual_high = residual_table.astype(jnp.bfloat16)
            residual_low = (residual_table - residual_high.astype(jnp.float32)).astype(
                jnp.bfloat16
            )
            residual_pair = jnp.concatenate([residual_high, residual_low], axis=0)
        own = own_v[...] if iteration == 0 else guess_v[iteration, mine]
        residual = jnp.dot(
            jnp.concatenate([own, own], axis=1), residual_pair, preferred_element_type=jnp.float32
        )
        partial = (step_size * partial).reshape(tensor_size, rows, channels)
        whole_v[...] = partial
        part_v[iteration] = partial.astype(jnp.bfloat16)
        drift = whole_v[mine] + step_size * residual
        part_v[iteration, mine] = drift.astype(jnp.bfloat16)

        def exchange(a, b):
            there = lax.rem(mine + b, tensor_size)
            slot = a * tensor_size + b
            return pltpu.make_async_remote_copy(
                src_ref=part_v.at[iteration, there],
                dst_ref=landed_v.at[iteration, slot],
                send_sem=part_send.at[iteration, slot],
                recv_sem=part_recv.at[iteration, slot],
                device_id={"tm": lax.rem(me + a, tm_size), "tensor": there},
                device_id_type=MESH,
            )

        for a, b in peers[::-1]:
            copy = exchange(a, b)
            copy.start()
            sends.append(copy)
        window = start_own
        for a, b in peers:
            exchange(a, b).wait_recv()
            arrived = landed_v[iteration, a * tensor_size + b].astype(jnp.float32)
            if a == 0:
                drift = drift + arrived
            else:
                window = window + jnp.where(a <= me, 1.0, 0.0) * arrived
        if iteration + 1 < ITERS:
            guess_v[iteration + 1, mine] = window.astype(jnp.bfloat16)
            later = iteration + 1
            sends += share(guess_v.at[later], guess_send.at[later], guess_recv.at[later])
            shared(guess_v.at[later], guess_send.at[later], guess_recv.at[later])
        else:
            o_ref[0] = window + drift
    for copy in sends:
        copy.wait_send()


def fused(tm_size, tensor_size, *arrays):
    start, _, _, in_w, mod_w, qkv_w, out_w, head_w = arrays
    rows, channels = start.shape
    bf16, f32 = jnp.bfloat16, jnp.float32
    dma = pltpu.SemaphoreType.DMA
    anywhere = pl.BlockSpec(memory_space=pl.ANY)
    vector = pl.BlockSpec(memory_space=pltpu.VMEM)
    return pl.pallas_call(
        lambda *refs: fused_kernel(tm_size, tensor_size, *refs),
        name="picard",
        out_shape=jax.ShapeDtypeStruct((1, rows, channels), f32),
        in_specs=[anywhere] * 8,
        out_specs=vector,
        scratch_shapes=[
            pltpu.VMEM(mod_w.shape, bf16),
            pltpu.VMEM(qkv_w.shape, bf16),
            pltpu.VMEM(out_w.shape, bf16),
            pltpu.VMEM((channels, D), bf16),
            pltpu.VMEM((D, channels), bf16),
            pltpu.VMEM((tensor_size, 1, mod_w.shape[1]), f32),
            pltpu.VMEM((channels, D), bf16),
            pltpu.VMEM((channels + 16, D), bf16),
            pltpu.VMEM((2 * channels, qkv_w.shape[1]), bf16),
            pltpu.VMEM((1, qkv_w.shape[1]), f32),
            pltpu.VMEM((out_w.shape[0], channels), bf16),
            pltpu.VMEM((ITERS, tensor_size, rows, channels), bf16),
            pltpu.VMEM((rows, channels), bf16),
            pltpu.VMEM((ITERS, tensor_size, rows, channels), bf16),
            pltpu.VMEM((ITERS, tm_size * tensor_size, rows, channels), bf16),
            pltpu.VMEM((tensor_size, rows, channels), f32),
            pltpu.VMEM((rows, channels), f32),
            pltpu.SMEM((1,), jnp.int32),
            pltpu.SMEM((1,), jnp.int32),
            dma((8,)),
            dma((tm_size,)),
            dma((tm_size,)),
            dma((tm_size,)),
            dma((tm_size,)),
            dma((tensor_size,)),
            dma((tensor_size,)),
            dma((ITERS, tensor_size)),
            dma((ITERS, tensor_size)),
            dma((ITERS, tm_size * tensor_size)),
            dma((ITERS, tm_size * tensor_size)),
        ],
        compiler_params=pltpu.CompilerParams(
            collective_id=0, has_side_effects=True, vmem_limit_bytes=67043328
        ),
    )(*arrays)


def aligned(tm_size, tensor_size, arrays):
    start, times, _, in_w, mod_w, qkv_w, out_w, head_w = arrays
    return (
        times.shape[0] == 1
        and tm_size % 2 == 0
        and in_w.shape[0] % 16 == 0
        and head_w.shape[0] % 16 == 0
        and start.shape[0] % 16 == 0
        and mod_w.shape[1] % 128 == 0
        and out_w.shape[0] % 128 == 0
    )


def device_program(tm_size, tensor_size):
    def run(*arrays):
        if aligned(tm_size, tensor_size, arrays):
            return fused(tm_size, tensor_size, *arrays)
        return local(*arrays)

    return run


def solution(mesh):
    return jax.shard_map(
        device_program(mesh.shape["tm"], mesh.shape["tensor"]),
        mesh=mesh,
        in_specs=(
            P(("groups", "tensor"), None),
            P(("groups", "tm")),
            P(("groups", "tm")),
            P("tm", None),
            P(None, "tensor"),
            P(None, "tensor"),
            P("tensor", None),
            P("tm", None),
        ),
        out_specs=P(("groups", "tm"), "tensor", None),
        check_vma=False,
    )
```
